32 devices in a mesh: dp: 8 (over y, x, core), seq: 4 (over z).
Axes of the slice: x: 2, y: 2, z: 4, core: 2. Of those that a mesh axis runs over, the one named last changes fastest.
Arguments:
- features: bfloat16 [8, 1024, 1024], P('dp', 'seq'), may hold values from -6 to 6
- shift_offsets: int32 [4], replicated, may hold values from -4 to 4, as said below
- conv_weight: bfloat16 [3, 1024, 1024], P(None, None, 'dp'), may hold values from -0.109375 to 0.109375
- norm_gain: float32 [1024], replicated, may hold values from 0.5 to 1.5
- query_proj: bfloat16 [8, 128, 512], P('dp', 'seq'), may hold values from -6 to 6
- key_proj: bfloat16 [8, 128, 512], P('dp', 'seq'), may hold values from -6 to 6
- value_proj: bfloat16 [8, 128, 768], P('dp', 'seq'), may hold values from -6 to 6
- head_weight: bfloat16 [1792, 512], replicated, may hold values from -0.125 to 0.125
- targets: float32 [8, 128, 512], P('dp', 'seq'), may hold values from 0 to 3
- track_mask: int32 [4, 512], replicated, may hold values from 0 to 1, as said below
- track_pairing: int32 [512], replicated, may hold values from 0 to 511, as said below
Outputs:
- features_grad: bfloat16 [8, 1024, 1024], P('dp', 'seq')
- query_grad: bfloat16 [8, 128, 512], P('dp', 'seq')
- key_grad: bfloat16 [8, 128, 512], P('dp', 'seq')
- value_grad: bfloat16 [8, 128, 768], P('dp', 'seq')
- gain_grad: float32 [1024], replicated
- mean_loss: float32 [], replicated
The draws below stay inside these ranges and needn't reach their ends.
Inputs may be any that keep to these rules, and one draw needn't show every extreme that they name: `shift_offsets`: offset in positions of each interval's 16-bp input. `track_mask`: 1 where the interval has data for the track. `track_pairing`: A pairing: applied twice it gives every track back.
All inputs are finite; a program needn't handle non-finite values.
Results may differ from the reference program's by a relative error of at most 0.028.
Values may be sent and summed in bfloat16 or wider, within the bound.
No kernel may reach another device: no remote copies, remote signals or barrier semaphores. Data moves between devices by JAX's collectives and lax.ppermute only.
A program may use at most 64 MiB of HBM per device.

```python
import math
from functools import partial
import jax
import jax.numpy as jnp
from jax import lax

C = 1024
KW = 3
SHIFT = 4
POOL = 8
HEADS = 4
QK = 128
VD = 192
TRACKS = 512
STRANDS = 8
INTERVALS = 4
L16 = 1024
L128 = 128


def draw_shift_offsets(key, part):
    seeded = jax.random.fold_in(key, 101)
    offsets = jax.random.randint(jax.random.fold_in(seeded, 1), (INTERVALS,), -SHIFT, SHIFT + 1)
    top_slot = jax.random.randint(jax.random.fold_in(seeded, 2), (), 0, INTERVALS)
    low_slot = (top_slot + 1 + jax.random.randint(jax.random.fold_in(seeded, 3), (), 0, INTERVALS - 1)) % INTERVALS
    offsets = offsets.at[top_slot].set(SHIFT)
    offsets = offsets.at[low_slot].set(-SHIFT)
    return offsets.astype(jnp.int32)


def draw_track_mask(key, part):
    seeded = jax.random.fold_in(key, 202)
    levels = jax.random.randint(jax.random.fold_in(seeded, 1), (INTERVALS, 1), 20, 91)
    dice_rolls = jax.random.randint(jax.random.fold_in(seeded, 2), (INTERVALS, TRACKS), 0, 100)
    empty_row = jax.random.randint(jax.random.fold_in(seeded, 3), (), 0, INTERVALS)
    kept_mask = (dice_rolls < levels) & (jnp.arange(INTERVALS)[:, None] != empty_row)
    return kept_mask.astype(jnp.int32)


def draw_track_pairing(key, part):
    seeded = jax.random.fold_in(key, 303)
    shuffled = jax.random.permutation(jax.random.fold_in(seeded, 1), TRACKS).astype(jnp.int32)
    unpaired = 2 * jax.random.randint(jax.random.fold_in(seeded, 2), (), 0, TRACKS // 4 + 1)
    slot_ids = jnp.arange(TRACKS, dtype=jnp.int32)
    mate_ids = slot_ids + 1 - 2 * (slot_ids % 2)
    mate_ids = jnp.where(slot_ids < unpaired, slot_ids, mate_ids)
    pairing = jnp.zeros((TRACKS,), jnp.int32).at[shuffled].set(shuffled[mate_ids])
    return pairing.astype(jnp.int32)


def draw_entries(key):
    seeded = jax.random.fold_in(key, 404)
    full_shape = (STRANDS, L128, HEADS * QK)
    queries = jax.random.truncated_normal(jax.random.fold_in(seeded, 1), -4.0, 4.0, full_shape, jnp.float32)
    keys_out = jax.random.truncated_normal(jax.random.fold_in(seeded, 2), -4.0, 4.0, full_shape, jnp.float32)
    return (queries, keys_out)


def draw_query_proj(key, part):
    return draw_entries(key)[0].astype(jnp.bfloat16)


def draw_key_proj(key, part):
    return draw_entries(key)[1].astype(jnp.bfloat16)


def block_scale(key, extent, pieces, smallest, high):
    loudness, own = 1.0, jax.random.fold_in(key, 6)
    for position, blocks in pieces:
        heights = jnp.exp(jax.random.uniform(jax.random.fold_in(own, position), (blocks,), jnp.float32, smallest / len(pieces), high / len(pieces)))
        loudness = loudness * jnp.repeat(heights, extent[position] // blocks).reshape([-1 if axis == position else 1 for axis in range(len(extent))])
    return loudness


def normal_values(rng, extent, spread, bound, shards=(), held_as=jnp.bfloat16):
    values = jax.random.normal(rng, extent, jnp.float32) * spread
    if len(shards) > 0:
        values = block_scale(rng, extent, shards, -0.22, 0.18) * values
    return jnp.clip(values, min=-bound, max=bound).astype(held_as)


def setup_inputs(seed: int = 0) -> dict:
    key_list = jax.random.split(jax.random.key(seed), 12)
    return {
        "features": normal_values(key_list[0], (STRANDS, L16, C), 1.0, 6.0, ((0, 8), (1, 4))),
        "shift_offsets": draw_shift_offsets(jax.random.fold_in(key_list[11], 71), 0),
        "conv_weight": normal_values(key_list[2], (KW, C, C), (KW * C) ** -0.5, 0.109375, ((2, 8),)),
        "norm_gain": jnp.clip(1.0 + 0.1 * jax.random.normal(key_list[3], (C,), jnp.float32), 0.5, 1.5),
        "query_proj": draw_query_proj(jax.random.fold_in(key_list[11], 71), 0),
        "key_proj": draw_key_proj(jax.random.fold_in(key_list[11], 71), 0),
        "value_proj": normal_values(key_list[6], (STRANDS, L128, HEADS * VD), 1.0, 6.0, ((0, 8), (1, 4))),
        "head_weight": normal_values(key_list[7], (C + HEADS * VD, TRACKS), (C + HEADS * VD) ** -0.5, 0.125),
        "targets": jnp.clip(3.0 * jax.random.uniform(key_list[8], (STRANDS, L128, TRACKS), jnp.float32) ** block_scale(key_list[8], (STRANDS, L128, TRACKS), ((0, 8), (1, 4)), -0.2, 0.2), 0.0, 3.0),
        "track_mask": draw_track_mask(jax.random.fold_in(key_list[11], 71), 0),
        "track_pairing": draw_track_pairing(jax.random.fold_in(key_list[11], 71), 0),
    }


NORM_EPS = 1e-06
LOSS_SCALE = 1024.0

def to_bfloat(values):
    return lax.optimization_barrier(values.astype(jnp.bfloat16)).astype(jnp.float32)

def normalize(feats_one, shift_one):
    length = feats_one.shape[0]
    padded = jnp.pad(feats_one, ((SHIFT, SHIFT), (0, 0)))
    shifted = lax.dynamic_slice_in_dim(padded, (SHIFT - shift_one).astype(jnp.int32), length, 0)
    source = shifted.astype(jnp.float32)
    inv_rms = lax.rsqrt(lax.optimization_barrier(jnp.mean(source * source, axis=1, keepdims=True)) + NORM_EPS)
    normed = source * inv_rms
    return (source, inv_rms, normed)

def pick_tap(conv_weight, flipped, tap_idx):
    tap_pick = jnp.where(flipped, KW - 1 - tap_idx, tap_idx).astype(jnp.int32)
    return lax.dynamic_index_in_dim(conv_weight, tap_pick, 0, keepdims=False)

def attend(query_one, key_one, value_one):
    query_h = query_one.astype(jnp.float32).reshape(-1, HEADS, QK)
    key_h = key_one.astype(jnp.float32).reshape(-1, HEADS, QK)
    value_h = value_one.astype(jnp.float32).reshape(-1, HEADS, VD)
    scores = jnp.einsum('thd,lhd->htl', query_h, key_h) * (1.0 / math.sqrt(QK))
    row_max = lax.optimization_barrier(jnp.max(scores, axis=2, keepdims=True))
    exp_scores = jnp.exp(scores - row_max)
    soft_f32 = exp_scores / lax.optimization_barrier(jnp.sum(exp_scores, axis=2, keepdims=True))
    soft_b16 = to_bfloat(soft_f32)
    attended = to_bfloat(jnp.einsum('htl,lhd->thd', soft_b16, value_h).reshape(-1, HEADS * VD))
    return (query_h, key_h, value_h, soft_f32, soft_b16, attended)

def predict(conv_weight, norm_gain, head_weight, packed):
    feats_one, shift_one, flipped, query_one, key_one, value_one = packed
    length = feats_one.shape[0]
    half_taps = KW // 2
    source, inv_rms, normed = normalize(feats_one, shift_one)
    hidden = jax.nn.gelu(normed * norm_gain).astype(jnp.bfloat16)
    hidden_pad = jnp.pad(hidden, ((half_taps, half_taps), (0, 0)))
    conv_out = jnp.zeros((length, C), jnp.float32)
    for tap_idx in range(KW):
        conv_out = conv_out + jnp.dot(hidden_pad[tap_idx:tap_idx + length], pick_tap(conv_weight, flipped, tap_idx), preferred_element_type=jnp.float32)
    output = to_bfloat(source + conv_out)
    pooled = lax.optimization_barrier(jnp.mean(output.reshape(length // POOL, POOL, C), axis=1)).astype(jnp.bfloat16)
    attended = attend(query_one, key_one, value_one)[5]
    joined = jnp.concatenate([pooled, attended.astype(jnp.bfloat16)], axis=1)
    return jnp.dot(joined, head_weight, preferred_element_type=jnp.float32)

def backprop(conv_weight, norm_gain, head_weight, packed):
    feats_one, shift_one, flipped, query_one, key_one, value_one, logits, dpred_one = packed
    length = feats_one.shape[0]
    half_taps = KW // 2
    source, inv_rms, normed = normalize(feats_one, shift_one)
    gained = normed * norm_gain
    query_h, key_h, value_h, soft_f32, soft_b16, attended = attend(query_one, key_one, value_one)
    dlogit = (dpred_one * jax.nn.sigmoid(logits)).astype(jnp.bfloat16)
    djoined = lax.dot_general(dlogit, head_weight, (((1,), (1,)), ((), ())), preferred_element_type=jnp.float32)
    dpooled = djoined[:, :C]
    dattended = to_bfloat(djoined[:, C:]).reshape(-1, HEADS, VD)
    row_dots = lax.optimization_barrier(jnp.sum(dattended * attended.reshape(-1, HEADS, VD), axis=2))
    dprobs = jnp.einsum('thd,lhd->htl', dattended, value_h)
    dscore = to_bfloat(soft_f32 * (dprobs - row_dots.T[:, :, None]))
    inv_sqrt = 1.0 / math.sqrt(QK)
    query_grad = (jnp.einsum('htl,lhd->thd', dscore, key_h) * inv_sqrt).reshape(-1, HEADS * QK).astype(jnp.bfloat16)
    key_grad = (jnp.einsum('htl,thd->lhd', dscore, query_h) * inv_sqrt).reshape(-1, HEADS * QK).astype(jnp.bfloat16)
    value_grad = jnp.einsum('htl,thd->lhd', soft_b16, dattended).reshape(-1, HEADS * VD).astype(jnp.bfloat16)
    dgrad_f32 = jnp.repeat(dpooled / POOL, POOL, axis=0)
    dgrad_pad = jnp.pad(dgrad_f32.astype(jnp.bfloat16), ((half_taps, half_taps), (0, 0)))
    dhidden = jnp.zeros((length, C), jnp.float32)
    for tap_idx in range(KW):
        tap_start = KW - 1 - tap_idx
        dhidden = dhidden + lax.dot_general(dgrad_pad[tap_start:tap_start + length], pick_tap(conv_weight, flipped, tap_idx), (((1,), (1,)), ((), ())), preferred_element_type=jnp.float32)
    unused, gelu_back = jax.vjp(jax.nn.gelu, gained)
    dgained = gelu_back(dhidden)[0]
    gain_part = lax.optimization_barrier(jnp.sum(dgained * normed, axis=0))
    dnormed = dgained * norm_gain
    dsource = inv_rms * (dnormed - normed * lax.optimization_barrier(jnp.mean(dnormed * normed, axis=1, keepdims=True))) + dgrad_f32
    dpadded = jnp.pad(dsource.astype(jnp.bfloat16), ((SHIFT, SHIFT), (0, 0)))
    features_grad = lax.dynamic_slice_in_dim(dpadded, (SHIFT + shift_one).astype(jnp.int32), length, 0)
    return (features_grad, query_grad, key_grad, value_grad, gain_part)

def reference(features, shift_offsets, conv_weight, norm_gain, query_proj, key_proj, value_proj, head_weight, targets, track_mask, track_pairing):
    signed = jnp.concatenate([shift_offsets, -shift_offsets]).astype(jnp.int32)
    flip_rows = jnp.arange(STRANDS) >= INTERVALS
    logits = lax.map(partial(predict, conv_weight, norm_gain, head_weight), (features, signed, flip_rows, query_proj, key_proj, value_proj))
    predicted = jax.nn.softplus(logits)
    mask_rows = jnp.concatenate([track_mask, track_mask], axis=0).astype(jnp.float32)
    counted = jnp.maximum(lax.optimization_barrier(jnp.sum(mask_rows, axis=1)), 1.0)[:, None, None]
    partner = jnp.roll(predicted, INTERVALS, axis=0)
    misfit = 0.5 * (predicted + jnp.take(partner, track_pairing, axis=2)) - targets
    weighted = mask_rows[:, None, :] * misfit
    mean_loss = jnp.sum(weighted * misfit / counted) / (STRANDS * L128)
    slopes = 2.0 * LOSS_SCALE * weighted / counted
    dpredicted = 0.5 * (slopes + jnp.take(jnp.roll(slopes, INTERVALS, axis=0), track_pairing, axis=2))
    gradients = lax.map(partial(backprop, conv_weight, norm_gain, head_weight), (features, signed, flip_rows, query_proj, key_proj, value_proj, logits, dpredicted))
    features_grad, query_grad, key_grad, value_grad, gain_parts = gradients
    return (features_grad, query_grad, key_grad, value_grad, lax.optimization_barrier(jnp.sum(gain_parts, axis=0)), mean_loss)
```

```python
import functools
import math

import jax
import jax.numpy as jnp
from jax import lax
from jax.experimental import pallas as pl
from jax.experimental.pallas import tpu as pltpu
from jax.sharding import PartitionSpec as P

KW = 3
SHIFT = 4
POOL = 8
HEADS = 4
QK = 128
VD = 192

NORM_EPS = 1e-06
LOSS_SCALE = 1024.0
GROUP = 4
EDGE = 16
CURVE = math.sqrt(2.0 / math.pi)
CUBIC = 0.044715
F32 = jnp.float32
BF16 = jnp.bfloat16
VMEM_MIB = 20


def call(kernel, outs, args, smem=0, scratch=()):
    whole = pl.BlockSpec(memory_space=pltpu.VMEM)
    return pl.pallas_call(
        kernel,
        out_shape=[jax.ShapeDtypeStruct(shape, dtype) for shape, dtype in outs],
        in_specs=[pl.BlockSpec(memory_space=pltpu.SMEM)] * smem + [whole] * (len(args) - smem),
        out_specs=[whole] * len(outs),
        scratch_shapes=list(scratch),
        compiler_params=pltpu.CompilerParams(vmem_limit_bytes=VMEM_MIB * 2**20),
    )(*args)


def dot(left, right, dims=((1,), (0,))):
    return lax.dot_general(left, right, (dims, ((), ())), preferred_element_type=F32)


def split3(value):
    first = value.astype(BF16)
    rest = value - first.astype(F32)
    second = rest.astype(BF16)
    third = (rest - second.astype(F32)).astype(BF16)
    return first, second, third


class Sizes:
    def __init__(self, features, track_mask):
        self.n = lax.axis_size("dp")
        self.seq = lax.axis_size("seq")
        self.rows = features.shape[1]
        self.chan = features.shape[2]
        self.tokens = self.rows // POOL
        self.ext = self.tokens + 16
        self.tracks = track_mask.shape[1]
        self.slice = self.chan // self.n
        self.wide = self.chan // GROUP
        self.sub = self.n // GROUP
        self.masks = (0, self.n // 4, self.n // 2, self.n // 2 + self.n // 4)


def place(sz, offs):
    me = lax.axis_index("dp")
    step = lax.axis_index("seq")
    half = sz.n // 2
    flipped = me >= half
    chosen = offs[lax.rem(me, half)]
    offset = jnp.where(flipped, -chosen, chosen)
    turn = jnp.where(flipped, -1, 1)
    return me, step, offset, turn


def token_of(sz, index):
    halo = jnp.where(index == sz.tokens, -1, jnp.where(index == sz.tokens + 1, sz.tokens, -(2**20)))
    return jnp.where(index < sz.tokens, index, halo)


def two_rows(low, high):
    shape = (16, low.shape[1])
    row = lax.broadcasted_iota(jnp.int32, shape, 0)
    return jnp.where(
        row == 0,
        jnp.broadcast_to(low, shape),
        jnp.where(row == 1, jnp.broadcast_to(high, shape), 0.0),
    )


def pack_kernel(sz, feats, query, key, value, targets, up, down, both):
    rows, tokens = sz.rows, sz.tokens
    both[:, : key.shape[1]] = key[...]
    both[:, key.shape[1] :] = value[...]
    for out, first, tok in ((up, rows - EDGE, tokens - 1), (down, 0, 0)):
        out[0:EDGE, :] = feats[first : first + EDGE, :]
        row = query[tok : tok + 1, :].astype(F32)
        want = targets[tok : tok + 1, :]
        high = want.astype(BF16).astype(F32)
        line = jnp.concatenate([row, jnp.zeros_like(row)], axis=1)
        line2 = jnp.concatenate([high, want - high], axis=1)
        out[EDGE : EDGE + 16, :] = two_rows(line, line2).astype(BF16)


def slice_kernel(sz, weight, *outs):
    me = lax.axis_index("dp")
    for k in range(sz.n):
        start = pl.multiple_of((me ^ k) * sz.slice, sz.slice)
        for tap in range(KW):
            outs[k][tap * sz.slice : (tap + 1) * sz.slice, :] = weight[
                tap, pl.ds(start, sz.slice), :
            ]


def merge_kernel(sz, head, *refs):
    me = lax.axis_index("dp")
    parts, out = refs[:-1], refs[-1]
    total = None
    for k in range(sz.n):
        start = pl.multiple_of((me ^ k) * sz.slice, sz.slice)
        term = dot(parts[k][...], head[pl.ds(start, sz.slice), :])
        total = term if total is None else total + term
    out[...] = total.astype(BF16)


def feature_kernel(
    sz, offs, feats, low, high, gain, buf0, buf1, buf2, buf3, ubar, slope, inv, exts, hs, gs, tiles
):
    me, step, offset, turn = place(sz, offs)
    rows, chan, ext, wide = sz.rows, sz.chan, sz.ext, sz.wide
    total = rows + 2 * EDGE
    exts[0:EDGE, :] = low[0:EDGE, :]
    exts[EDGE : EDGE + rows, :] = feats[...]
    exts[EDGE + rows :, :] = high[0:EDGE, :]
    scale = gain[...]

    def chunk(index, carry):
        at = pl.ds(pl.multiple_of(index * 16, 16), 16)
        source = exts[at, :].astype(F32)
        rms = lax.rsqrt(jnp.mean(source * source, axis=1, keepdims=True) + NORM_EPS)
        normed = source * rms
        g = normed * scale
        square = g * g
        curve = jnp.tanh(CURVE * g * (1.0 + CUBIC * square))
        half = 0.5 * (1.0 + curve)
        hs[at, :] = (g * half).astype(BF16)
        dgelu = half + 0.5 * CURVE * g * (1.0 - curve * curve) * (1.0 + 3.0 * CUBIC * square)
        gs[at, :] = (dgelu * normed).astype(BF16)
        slope[at, :] = dgelu * scale
        inv[at, :] = jnp.broadcast_to(rms, (16, 128))
        return carry

    lax.fori_loop(0, total // 16, chunk, 0)
    shape = (ext, total)
    token = token_of(sz, lax.broadcasted_iota(jnp.int32, shape, 0))
    spot = lax.broadcasted_iota(jnp.int32, shape, 1) - EDGE + offset
    inside = (spot + step * rows >= 0) & (spot + step * rows < sz.seq * rows)
    picks = []
    for tap in range(KW):
        hit = (((spot - turn * (tap - KW // 2)) >> 3) == token) & inside
        picks.append(jnp.where(hit, 1.0 / POOL, 0.0).astype(BF16))
    ubar[...] = dot(picks[KW // 2], exts[...]).astype(BF16)
    for tap in range(KW):
        held = dot(picks[tap], hs[...]).astype(BF16)
        grad = dot(picks[tap][: sz.tokens], gs[...]).astype(BF16)
        for part in range(GROUP):
            lanes = slice(part * wide, (part + 1) * wide)
            tiles[part, 0:ext, tap * wide : (tap + 1) * wide] = held[:, lanes]
            tiles[part, ext:, tap * wide : (tap + 1) * wide] = grad[:, lanes]
    for out, mask in zip((buf0, buf1, buf2, buf3), sz.masks):
        out[...] = tiles[(me ^ mask) // sz.sub]


def attend_kernel(sz, query, low, high, targets, ubar, head, *refs):
    parts = refs[: sz.seq]
    probs, attended, own, wanted = refs[sz.seq :]
    chan, tokens = sz.chan, sz.tokens
    wide = HEADS * QK
    edge = two_rows(
        low[EDGE : EDGE + 16, :].astype(F32)[0:1], high[EDGE : EDGE + 16, :].astype(F32)[0:1]
    )
    edge2 = two_rows(
        low[EDGE : EDGE + 16, :].astype(F32)[1:2], high[EDGE : EDGE + 16, :].astype(F32)[1:2]
    )
    wanted[0:tokens, :] = targets[...]
    wanted[tokens:, :] = edge2[:, : sz.tracks] + edge2[:, sz.tracks :]
    asks = jnp.concatenate([query[...], edge[:, :wide].astype(BF16)], axis=0)
    keys = jnp.concatenate([part[:, :wide] for part in parts], axis=0)
    values = jnp.concatenate([part[:, wide:] for part in parts], axis=0)
    inv_sqrt = 1.0 / math.sqrt(QK)
    logits = dot(ubar[...], head[0:chan, :])
    for pair in range(HEADS // 2):
        lanes = slice(pair * 2 * VD, (pair + 1) * 2 * VD)
        outs = []
        for one in range(2):
            head_at = pair * 2 + one
            cols = slice(head_at * QK, (head_at + 1) * QK)
            scores = dot(asks[:, cols], keys[:, cols], ((1,), (1,))) * inv_sqrt
            exps = jnp.exp(scores - jnp.max(scores, axis=1, keepdims=True))
            soft = exps / jnp.sum(exps, axis=1, keepdims=True)
            probs[head_at] = soft[:tokens]
            outs.append(dot(soft.astype(BF16), values[:, lanes]))
        lane = lax.broadcasted_iota(jnp.int32, outs[0].shape, 1)
        seen = jnp.where(lane < VD, outs[0], outs[1]).astype(BF16)
        attended[:, lanes] = seen[:tokens]
        start = chan + pair * 2 * VD
        logits = logits + dot(seen, head[start : start + 2 * VD, :])
    own[...] = logits


def logits_kernel(sz, extra, *refs):
    bufs, parts = refs[:GROUP], refs[GROUP : GROUP + sz.sub]
    mine, near, far, merged = refs[GROUP + sz.sub :]
    spot = lax.rem(lax.axis_index("dp"), sz.sub)
    for k in range(sz.sub):
        for tap in range(KW):
            start = pl.multiple_of(tap * sz.wide + (spot ^ k) * sz.slice, sz.slice)
            merged[pl.ds(start, sz.slice), :] = parts[k][
                tap * sz.slice : (tap + 1) * sz.slice, :
            ]
    ext = sz.ext
    weight = merged[...]
    own = dot(bufs[0][0:ext, :], weight) + extra[...]
    partner = dot(bufs[2][0:ext, :], weight)
    mine[0:ext, :] = own
    mine[ext:, :] = partner
    near[0:ext, :] = own.astype(BF16)
    near[ext:, :] = partner.astype(BF16)
    far[0:ext, :] = dot(bufs[1][0:ext, :], weight).astype(BF16)
    far[ext:, :] = dot(bufs[3][0:ext, :], weight).astype(BF16)


def loss_kernel(sz, mine, fa, fb, fab, want, want2, mask, pairing, dlogit, loss):
    me = lax.axis_index("dp")
    step = lax.axis_index("seq")
    ext, tracks = sz.ext, sz.tracks
    f = lambda ref, at: ref[at * ext : (at + 1) * ext, :].astype(F32)
    first = f(mine, 0) + f(fa, 0) + f(fb, 1) + f(fab, 1)
    second = f(mine, 1) + f(fa, 1) + f(fb, 0) + f(fab, 0)
    logit = jnp.concatenate([first, second], axis=0)
    decay = jnp.exp(-jnp.abs(logit))
    pred = jnp.maximum(logit, 0.0) + jnp.log1p(decay)
    sigmoid = jnp.where(logit >= 0.0, 1.0, decay) / (1.0 + decay)
    square = (tracks, tracks)
    move = (lax.broadcasted_iota(jnp.int32, square, 0) == pairing[...]).astype(F32).astype(BF16)
    rows = lax.broadcasted_iota(jnp.int32, mask.shape, 0)
    interval = lax.rem(me, sz.n // 2)
    kept = jnp.sum(jnp.where(rows == interval, mask[...], 0), axis=0, keepdims=True).astype(F32)
    kept2 = dot(jnp.broadcast_to(kept, (16, tracks)).astype(BF16), move)[0:1]
    count = jnp.maximum(jnp.sum(kept, axis=1, keepdims=True), 1.0)

    def moved(value):
        return sum(dot(part, move) for part in split3(value))

    both = jnp.concatenate([want[...], want2[...]], axis=0)
    pred_m = moved(pred)
    both_m = moved(both)
    swap = lambda x: jnp.concatenate([x[ext:], x[:ext]], axis=0)
    misfit = 0.5 * (pred + swap(pred_m)) - both
    misfit2 = swap(0.5 * (pred_m + swap(pred)) - both_m)
    dpred = (LOSS_SCALE / count) * (kept * misfit + kept2 * misfit2)
    row = lax.broadcasted_iota(jnp.int32, (2 * ext, tracks), 0)
    row = jnp.where(row >= ext, row - ext, row)
    token = token_of(sz, row) + step * sz.tokens
    fine = (token >= 0) & (token < sz.seq * sz.tokens)
    dlogit[...] = jnp.where(fine, dpred * sigmoid, 0.0).astype(BF16)
    own = misfit[: sz.tokens]
    part = jnp.sum(kept * own * own, axis=0, keepdims=True)
    part = jnp.sum(part, axis=1, keepdims=True) / count
    loss[...] = jnp.broadcast_to(part * (1.0 / (sz.n * sz.tokens * sz.seq)), loss.shape)


def spread_kernel(sz, grad, grad2, merged, loss, *refs):
    bufs = refs[:GROUP]
    outs = refs[GROUP : 2 * GROUP]
    totals = refs[2 * GROUP]
    ext, tokens, wide = sz.ext, sz.tokens, sz.wide
    weight = merged[...]
    total = None
    for at, (source, row) in enumerate(((grad, 0), (grad2, 0), (grad, ext), (grad2, ext))):
        back = dot(source[row : row + ext, :], weight, ((1,), (1,)))
        outs[at][...] = back.astype(BF16)
        term = back[:tokens] * bufs[at][ext:, :].astype(F32)
        total = term if total is None else total + term
    total = jnp.sum(total, axis=0, keepdims=True)
    line = total[:, :wide]
    for tap in range(1, KW):
        line = line + total[:, tap * wide : (tap + 1) * wide]
    line = jnp.concatenate([line, loss[0:1, :]], axis=1)
    totals[...] = jnp.broadcast_to(line, totals.shape)


def attend_back_kernel(sz, grad, head, query, probs, attended, *refs):
    parts = refs[: sz.seq]
    dquery, dpool, mine = refs[sz.seq : sz.seq + 3]
    sends = refs[sz.seq + 3 :]
    tokens, chan = sz.tokens, sz.chan
    wide = HEADS * QK
    inv_sqrt = 1.0 / math.sqrt(QK)
    dpool[...] = dot(grad[0 : sz.ext, :], head[0:chan, :], ((1,), (1,))).astype(BF16)
    dout = dot(grad[0:tokens, :], head[chan:, :], ((1,), (1,))).astype(BF16)
    keys = jnp.concatenate([part[:, :wide] for part in parts], axis=0)
    values = jnp.concatenate([part[:, wide:] for part in parts], axis=0)

    def emit(value, start):
        stop = start + value.shape[1]
        mine[:, start:stop] = value[0:tokens]
        for k in range(1, sz.seq):
            sends[k - 1][:, start:stop] = value[k * tokens : (k + 1) * tokens].astype(BF16)

    for pair in range(HEADS // 2):
        lanes = slice(pair * 2 * VD, (pair + 1) * 2 * VD)
        given = dout[:, lanes]
        lane = lax.broadcasted_iota(jnp.int32, given.shape, 1)
        outs = []
        for one in range(2):
            head_at = pair * 2 + one
            cols = slice(head_at * QK, (head_at + 1) * QK)
            here = (lane < VD) if one == 0 else (lane >= VD)
            part = jnp.where(here, given.astype(F32), 0.0)
            delta = jnp.sum(part * attended[:, lanes].astype(F32), axis=1, keepdims=True)
            dprobs = dot(part.astype(BF16), values[:, lanes], ((1,), (1,)))
            soft = probs[head_at]
            dscore = (soft * (dprobs - delta)).astype(BF16)
            dquery[:, cols] = (dot(dscore, keys[:, cols]) * inv_sqrt).astype(BF16)
            emit(dot(dscore, query[:, cols], ((0,), (0,))) * inv_sqrt, head_at * QK)
            outs.append(dot(soft.astype(BF16), given, ((0,), (0,))))
        lane = lax.broadcasted_iota(jnp.int32, outs[0].shape, 1)
        emit(jnp.where(lane < VD, outs[0], outs[1]), wide + pair * 2 * VD)


def final_kernel(sz, offs, feats, slope, inv, dpool, z0, z1, z2, z3, out, joined, dhs, dys):
    me, step, offset, turn = place(sz, offs)
    rows, ext, wide = sz.rows, sz.ext, sz.wide
    for ref, mask in zip((z0, z1, z2, z3), sz.masks):
        at = (me ^ mask) // sz.sub
        for tap in range(KW):
            joined[at, tap * ext : (tap + 1) * ext, :] = ref[:, tap * wide : (tap + 1) * wide]
    shape = (rows, ext)
    spot = lax.broadcasted_iota(jnp.int32, shape, 0) + offset
    token = token_of(sz, lax.broadcasted_iota(jnp.int32, shape, 1))
    picks = []
    for tap in range(KW):
        hit = ((spot - turn * (tap - KW // 2)) >> 3) == token
        picks.append(jnp.where(hit, 1.0 / POOL, 0.0).astype(BF16))
    dys[...] = dot(picks[KW // 2], dpool[...])
    for part in range(GROUP):
        total = None
        for tap in range(KW):
            term = dot(picks[tap], joined[part, tap * ext : (tap + 1) * ext, :])
            total = term if total is None else total + term
        dhs[:, part * wide : (part + 1) * wide] = total

    def chunk(index, carry):
        start = pl.multiple_of(index * 16, 16)
        at = pl.ds(start, 16)
        at2 = pl.ds(start + EDGE, 16)
        rms = inv[at2, :][:, 0:1]
        normed = feats[at, :].astype(F32) * rms
        dnormed = dhs[at, :] * slope[at2, :]
        along = jnp.mean(dnormed * normed, axis=1, keepdims=True)
        du = rms * (dnormed - normed * along) + dys[at, :]
        place_at = lax.broadcasted_iota(jnp.int32, du.shape, 0) + (start + offset + step * rows)
        fine = (place_at >= 0) & (place_at < sz.seq * rows)
        out[at, :] = jnp.where(fine, du, 0.0).astype(BF16)
        return carry

    lax.fori_loop(0, rows // 16, chunk, 0)


def sum_kernel(sz, mine, *refs):
    key_grad, value_grad = refs[-2:]
    total = mine[...]
    for ref in refs[:-2]:
        total = total + ref[...].astype(F32)
    wide = HEADS * QK
    key_grad[...] = total[:, :wide].astype(BF16)
    value_grad[...] = total[:, wide:].astype(BF16)


def swapped(value, mask):
    return lax.ppermute(value, "dp", [(i, i ^ mask) for i in range(lax.axis_size("dp"))])


def rotated(value, shift):
    count = lax.axis_size("seq")
    return lax.ppermute(value, "seq", [(i, (i + shift) % count) for i in range(count)])


def body(
    features,
    shift_offsets,
    conv_weight,
    norm_gain,
    query_proj,
    key_proj,
    value_proj,
    head_weight,
    targets,
    track_mask,
    track_pairing,
):
    sz = Sizes(features, track_mask)
    bind = lambda kernel: functools.partial(kernel, sz)
    n, seq, tokens, ext, chan = sz.n, sz.seq, sz.tokens, sz.ext, sz.chan
    rows, tracks, wide = sz.rows, sz.tracks, sz.wide
    feats, query, wanted = features[0], query_proj[0], targets[0]
    kv_wide = key_proj.shape[2] + value_proj.shape[2]

    up, down, both = call(
        bind(pack_kernel),
        [((2 * EDGE, chan), BF16), ((2 * EDGE, chan), BF16), ((tokens, kv_wide), BF16)],
        [feats, query, key_proj[0], value_proj[0], wanted],
    )
    low = lax.ppermute(up, "seq", [(i, i + 1) for i in range(seq - 1)])
    high = lax.ppermute(down, "seq", [(i + 1, i) for i in range(seq - 1)])
    pieces = call(
        bind(slice_kernel),
        [((KW * sz.slice, conv_weight.shape[2]), BF16)] * n,
        [conv_weight],
    )
    pieces = [pieces[0]] + [swapped(pieces[k], k) for k in range(1, n)]
    blocks = [both] + [rotated(both, k) for k in range(1, seq)]

    outs = call(
        bind(feature_kernel),
        [((ext + tokens, KW * wide), BF16)] * GROUP
        + [((ext, chan), BF16), ((rows + 2 * EDGE, chan), F32), ((rows + 2 * EDGE, 128), F32)],
        [shift_offsets, feats, low, high, norm_gain[None]],
        smem=1,
        scratch=[
            pltpu.VMEM((rows + 2 * EDGE, chan), BF16),
            pltpu.VMEM((rows + 2 * EDGE, chan), BF16),
            pltpu.VMEM((rows + 2 * EDGE, chan), BF16),
            pltpu.VMEM((GROUP, ext + tokens, KW * wide), BF16),
        ],
    )
    bufs, (ubar, slope, inv) = outs[:GROUP], outs[GROUP:]
    bufs = [bufs[0]] + [swapped(bufs[k], sz.masks[k]) for k in range(1, GROUP)]

    probs, attended, extra, want = call(
        bind(attend_kernel),
        [
            ((HEADS, tokens, seq * tokens), F32),
            ((tokens, HEADS * VD), BF16),
            ((ext, tracks), F32),
            ((ext, tracks), F32),
        ],
        [query, low, high, wanted, ubar, head_weight] + blocks,
    )
    want2 = swapped(want, n // 2)

    merged = call(bind(merge_kernel), [((KW * sz.slice, tracks), BF16)], [head_weight] + pieces)[0]
    merged = [merged] + [swapped(merged, k) for k in range(1, sz.sub)]

    mine, near, far, weight = call(
        bind(logits_kernel),
        [
            ((2 * ext, tracks), F32),
            ((2 * ext, tracks), BF16),
            ((2 * ext, tracks), BF16),
            ((KW * wide, tracks), BF16),
        ],
        [extra] + bufs + merged,
    )
    fa = swapped(far, sz.masks[1])
    fb = swapped(near, sz.masks[2])
    fab = swapped(far, sz.masks[3])

    grad, loss = call(
        bind(loss_kernel),
        [((2 * ext, tracks), BF16), ((8, 128), F32)],
        [mine, fa, fb, fab, want, want2, track_mask, track_pairing[None]],
    )
    grad2 = swapped(grad, sz.masks[1])

    outs = call(
        bind(spread_kernel),
        [((ext, KW * wide), BF16)] * GROUP + [((8, wide + 128), F32)],
        [grad, grad2, weight, loss] + bufs,
    )
    spread, totals = outs[:GROUP], outs[GROUP]
    spread = [spread[0]] + [swapped(spread[k], sz.masks[k]) for k in range(1, GROUP)]
    shared = lax.all_to_all(
        jnp.broadcast_to(totals[0:1], (n * seq, wide + 128)), ("dp", "seq"), 0, 0, tiled=True
    )
    shared = jnp.sum(shared.reshape(GROUP, -1, wide + 128), axis=1)
    gain_grad = shared[:, :wide].reshape(chan)
    mean_loss = jnp.sum(shared[:, wide])

    outs = call(
        bind(attend_back_kernel),
        [((tokens, HEADS * QK), BF16), ((ext, chan), BF16), ((tokens, kv_wide), F32)]
        + [((tokens, kv_wide), BF16)] * (seq - 1),
        [grad, head_weight, query, probs, attended] + blocks,
    )
    query_grad, dpool, own_kv = outs[:3]
    kv_parts = [rotated(outs[2 + k], -k) for k in range(1, seq)]

    features_grad = call(
        bind(final_kernel),
        [((rows, chan), BF16)],
        [shift_offsets, feats, slope, inv, dpool] + spread,
        smem=1,
        scratch=[
            pltpu.VMEM((GROUP, KW * ext, wide), BF16),
            pltpu.VMEM((rows, chan), F32),
            pltpu.VMEM((rows, chan), F32),
        ],
    )[0]
    key_grad, value_grad = call(
        bind(sum_kernel),
        [((tokens, HEADS * QK), BF16), ((tokens, HEADS * VD), BF16)],
        [own_kv] + kv_parts,
    )
    return (
        features_grad[None],
        query_grad[None],
        key_grad[None],
        value_grad[None],
        gain_grad,
        mean_loss,
    )


def solution(mesh):
    split = P("dp", "seq", None)
    return jax.shard_map(
        body,
        mesh=mesh,
        in_specs=(split, P(), P(None, None, "dp"), P(), split, split, split, P(), split, P(), P()),
        out_specs=(split, split, split, split, P(), P()),
        check_vma=False,
    )
```
